32 devices in a mesh: fsdp: 4 (over z), ctx: 4 (over x, core), tp: 2 (over y).
Axes of the slice: x: 2, y: 2, z: 4, core: 2. Of those that a mesh axis runs over, the one named last changes fastest.
Arguments:
- block_input: bfloat16 [2, 4, 4096, 768], P(None, 'fsdp', 'ctx'), may hold values from -6 to 6
- ln1_gain: bfloat16 [768], P('fsdp'), may hold values from 0.5 to 1.5
- ln1_bias: bfloat16 [768], P('fsdp'), may hold values from -0.29882812 to 0.29882812
- w_qkv: bfloat16 [768, 3, 768], P('fsdp', None, 'tp'), may hold values from -0.21875 to 0.21875
- w_feature: bfloat16 [12, 64, 64], P('tp', 'fsdp'), may hold values from -0.75 to 0.75
- w_out: bfloat16 [768, 768], P('tp', 'fsdp'), may hold values from -1.5 to 1.5
- ln2_gain: bfloat16 [768], P('fsdp'), may hold values from 0.5 to 1.5
- ln2_bias: bfloat16 [768], P('fsdp'), may hold values from -0.29882812 to 0.29882812
- w_up: bfloat16 [768, 3072], P('fsdp', 'tp'), may hold values from -0.21875 to 0.21875
- w_down: bfloat16 [3072, 768], P('tp', 'fsdp'), may hold values from -0.109375 to 0.109375
- cotangent: bfloat16 [2, 4, 4096, 768], P(None, 'fsdp', 'ctx'), may hold values from -6 to 6
Outputs:
- block_output: bfloat16 [2, 4, 4096, 768], P(None, 'fsdp', 'ctx')
- grad_input: bfloat16 [2, 4, 4096, 768], P(None, 'fsdp', 'ctx')
- grad_ln1_gain: float32 [768], P('fsdp')
- grad_ln1_bias: float32 [768], P('fsdp')
- grad_qkv: float32 [768, 3, 768], P('fsdp', None, 'tp')
- grad_feature: float32 [12, 64, 64], P('tp', 'fsdp')
- grad_out: float32 [768, 768], P('tp', 'fsdp')
- grad_ln2_gain: float32 [768], P('fsdp')
- grad_ln2_bias: float32 [768], P('fsdp')
- grad_up: float32 [768, 3072], P('fsdp', 'tp')
- grad_down: float32 [3072, 768], P('tp', 'fsdp')
The draws below stay inside these ranges and needn't reach their ends.
All inputs are finite; a program needn't handle non-finite values.
Results may differ from the reference program's by a relative error of at most 0.02.
Values may be sent and summed in bfloat16 or wider, within the bound.
No kernel may reach another device: no remote copies, remote signals or barrier semaphores. Data moves between devices by JAX's collectives and lax.ppermute only.
A program may use at most 256 MiB of HBM per device.

```python
import jax
import jax.numpy as jnp
from jax import lax

D = 768
HEADS = 12
HEAD_DIM = 64
FF = 3072
FEATURES = 128
SPAN = 64
SEQ_LEN = 4096
MB = 2
SEQS = 4


def steps_of(stream_key, dims, pieces, least, high):
    level, own = 1.0, jax.random.fold_in(stream_key, 6)
    for axis_at, parts in pieces:
        heights = jnp.exp(jax.random.uniform(jax.random.fold_in(own, axis_at), (parts,), jnp.float32, least / len(pieces), high / len(pieces)))
        level = level * jnp.repeat(heights, dims[axis_at] // parts).reshape([-1 if axis == axis_at else 1 for axis in range(len(dims))])
    return level


def gaussian(stream_key, dims, width, bound, cuts=(), kind=jnp.bfloat16):
    drawn = jax.random.normal(stream_key, dims, jnp.float32) * width
    if len(cuts) > 0:
        drawn = steps_of(stream_key, dims, cuts, -0.22, 0.18) * drawn
    return jnp.clip(drawn, min=-bound, max=bound).astype(kind)


def setup_inputs(seed: int = 0) -> dict:
    streams_of = jax.random.split(jax.random.key(seed), 12)
    return {
        "block_input": gaussian(streams_of[0], (MB, SEQS, SEQ_LEN, D), 1.0, 6.0, ((1, 4), (2, 4))),
        "ln1_gain": jnp.clip(1.0 + 0.1 * jax.random.normal(streams_of[1], (D,), jnp.float32), 0.5, 1.5).astype(jnp.bfloat16),
        "ln1_bias": jnp.clip(jax.random.uniform(streams_of[2], (D,), jnp.float32, -0.29882812, 0.29882812) * steps_of(streams_of[2], (D,), ((0, 4),), -0.4, 0.0), -0.29882812, 0.29882812).astype(jnp.bfloat16),
        "w_qkv": gaussian(streams_of[3], (D, 3, D), D ** -0.5, 0.21875, ((0, 4), (2, 2))),
        "w_feature": gaussian(streams_of[4], (HEADS, HEAD_DIM, HEAD_DIM), HEAD_DIM ** -0.5, 0.75, ((0, 2), (1, 4))),
        "w_out": gaussian(streams_of[5], (D, D), (HEAD_DIM // 4) ** -0.5, 1.5, ((0, 2), (1, 4))),
        "ln2_gain": jnp.clip(1.0 + 0.1 * jax.random.normal(streams_of[6], (D,), jnp.float32), 0.5, 1.5).astype(jnp.bfloat16),
        "ln2_bias": jnp.clip(jax.random.uniform(streams_of[7], (D,), jnp.float32, -0.29882812, 0.29882812) * steps_of(streams_of[7], (D,), ((0, 4),), -0.4, 0.0), -0.29882812, 0.29882812).astype(jnp.bfloat16),
        "w_up": gaussian(streams_of[8], (D, FF), D ** -0.5, 0.21875, ((0, 4), (1, 2))),
        "w_down": gaussian(streams_of[9], (FF, D), FF ** -0.5, 0.109375, ((0, 2), (1, 4))),
        "cotangent": gaussian(streams_of[10], (MB, SEQS, SEQ_LEN, D), 1.0, 6.0, ((1, 4), (2, 4))),
    }


EPSILON = 1e-05
HIGHEST = lax.Precision.HIGHEST

@jax.custom_vjp
def low(v):
    return lax.optimization_barrier(v.astype(jnp.bfloat16)).astype(jnp.float32)

@jax.custom_vjp
def low_back(v):
    return v

def low_keep(v):
    return (low(v), None)

def low_pass(kept, grad):
    return (grad,)

def back_keep(v):
    return (v, None)

def back_low(kept, grad):
    return (low(grad),)
low.defvjp(low_keep, low_pass)
low_back.defvjp(back_keep, back_low)

def layer_norm(values, gain, shift):
    centre = values - lax.optimization_barrier(jnp.mean(values, -1, keepdims=True))
    scaled = centre * lax.rsqrt(lax.optimization_barrier(jnp.mean(centre * centre, -1, keepdims=True)) + EPSILON)
    return scaled * gain + shift

def feature_map(inner):
    return jnp.concatenate([jax.nn.softmax(inner, -1), jax.nn.softmax(-inner, -1)], -1)

def exclusive(arrays):
    totals = jnp.cumsum(arrays, 0)
    return jnp.concatenate([jnp.zeros_like(arrays[:1]), totals[:-1]], 0)

def block_forward(inputs, gain_one, shift_one, w_qkv, w_feature, w_out, gain_two, shift_two, w_up, w_down):
    length = inputs.shape[0]
    blocks = length // SPAN
    normed = low(layer_norm(inputs, gain_one, shift_one))
    projected = jnp.dot(normed, w_qkv.reshape(D, 3 * D), precision=HIGHEST)
    projected = low(low_back(projected)).reshape(length, 3, HEADS, HEAD_DIM)

    def featurize(rows_in):
        inner = jnp.einsum('thd,hde->the', rows_in, w_feature, precision=HIGHEST)
        return low(feature_map(inner)).reshape(blocks, SPAN, HEADS, FEATURES)
    phi_query = featurize(projected[:, 0])
    phi_key = featurize(projected[:, 1])
    value_rows = projected[:, 2].reshape(blocks, SPAN, HEADS, HEAD_DIM)
    causal = (jnp.arange(SPAN)[:, None] >= jnp.arange(SPAN)[None, :]).astype(jnp.float32)
    scores = jnp.einsum('cihf,cjhf->chij', phi_query, phi_key, precision=HIGHEST) * causal
    states = jnp.einsum('cjhf,cjhd->chfd', phi_key, value_rows, precision=HIGHEST)
    earlier = exclusive(states)
    earlier_sum = exclusive(lax.optimization_barrier(jnp.sum(phi_key, 1)))
    numer = jnp.einsum('cihf,chfd->cihd', phi_query, earlier, precision=HIGHEST)
    numer = numer + jnp.einsum('chij,cjhd->cihd', scores, value_rows, precision=HIGHEST)
    denom = jnp.einsum('cihf,chf->cih', phi_query, earlier_sum, precision=HIGHEST)
    denom = denom + jnp.transpose(lax.optimization_barrier(jnp.sum(scores, -1)), (0, 2, 1))
    mixed = low(low_back(numer / denom[..., None])).reshape(length, D)
    attended = low_back(jnp.dot(mixed, w_out, precision=HIGHEST))
    middle = inputs + attended
    normed_two = low(layer_norm(middle, gain_two, shift_two))
    upper = low_back(jnp.dot(normed_two, w_up, precision=HIGHEST))
    hidden = low(jax.nn.gelu(upper, approximate=True))
    return middle + low_back(jnp.dot(hidden, w_down, precision=HIGHEST))

def reference(block_input, ln1_gain, ln1_bias, w_qkv, w_feature, w_out, ln2_gain, ln2_bias, w_up, w_down, cotangent):
    weights = tuple((item.astype(jnp.float32) for item in (ln1_gain, ln1_bias, w_qkv, w_feature, w_out, ln2_gain, ln2_bias, w_up, w_down)))
    count = MB * SEQS
    inputs = block_input.astype(jnp.float32).reshape(count, SEQ_LEN, D)
    cotangents = cotangent.astype(jnp.float32).reshape(count, SEQ_LEN, D)

    def one_sequence(totals, paired):
        output, pullback = jax.vjp(block_forward, paired[0], *weights)
        grads = pullback(paired[1])
        summed = tuple((total + grad for total, grad in zip(totals, grads[1:])))
        return (summed, (output, grads[0]))
    start = tuple((jnp.zeros_like(item) for item in weights))
    totals, results = lax.scan(one_sequence, start, (inputs, cotangents))
    outputs, grad_inputs = results
    layout = block_input.shape
    return (outputs.reshape(layout).astype(jnp.bfloat16), grad_inputs.reshape(layout).astype(jnp.bfloat16), totals[0], totals[1], totals[2], totals[3], totals[4], totals[5], totals[6], totals[7], totals[8])
```

```python
from functools import partial

import jax
import jax.numpy as jnp
from jax import lax
from jax.experimental import pallas as pl
from jax.experimental.pallas import tpu as pltpu
from jax.sharding import PartitionSpec as P

EPSILON = 1e-05
TILE = 256
HEAD = 64
FEAT = 128
LANES = 128
BF = jnp.bfloat16
F32 = jnp.float32
ROOT = 0.7978845608028654
CUBIC = 0.044715
VMEM_LIMIT = 60 * 1024 * 1024


def nn(a, b):
    return lax.dot_general(a, b, (((1,), (0,)), ((), ())), preferred_element_type=F32)


def nt(a, b):
    return lax.dot_general(a, b, (((1,), (1,)), ((), ())), preferred_element_type=F32)


def tn(a, b):
    return lax.dot_general(a, b, (((0,), (0,)), ((), ())), preferred_element_type=F32)


def lanes_of(shape):
    return lax.broadcasted_iota(jnp.int32, shape, len(shape) - 1)


def group_ones():
    rows = lax.broadcasted_iota(jnp.int32, (2 * LANES, 2 * LANES), 0) // HEAD
    cols = lax.broadcasted_iota(jnp.int32, (2 * LANES, 2 * LANES), 1) // HEAD
    return (rows == cols).astype(BF)


def normalized(values):
    centre = values - jnp.mean(values, -1, keepdims=True)
    inverse = lax.rsqrt(jnp.mean(centre * centre, -1, keepdims=True) + EPSILON)
    return centre * inverse, inverse


def norm_back(incoming, scaled, inverse, gain):
    weighted = incoming * gain
    return inverse * (
        weighted
        - jnp.mean(weighted, -1, keepdims=True)
        - scaled * jnp.mean(weighted * scaled, -1, keepdims=True)
    )


def row_sums(values):
    return jnp.sum(values.reshape(values.shape[0] // 8, 8, values.shape[1]), 0)


def pack_states(get, put, pairs, left):
    cols = lanes_of((FEAT, LANES))
    sums = jnp.zeros((FEAT, LANES), F32)
    for p in range(pairs):
        even, odd = get(2 * p), get(2 * p + 1)
        put(p, jnp.where(left, even, odd))
        sums = jnp.where(cols == HEAD + 2 * p, even, sums)
        sums = jnp.where(cols == 2 * p + 1, odd, sums)
    put(pairs, sums)


def unpack_states(get, put, pairs, left):
    sums = get(pairs)
    for p in range(pairs):
        both = get(p)
        put(2 * p, jnp.where(left, both, sums[:, HEAD + 2 * p : HEAD + 2 * p + 1]))
        put(2 * p + 1, jnp.where(left, sums[:, 2 * p + 1 : 2 * p + 2], both))


def fetch(sp, pieces, jobs, sem, parts, do):
    for at, (piece, (step, other_y, other_c)) in enumerate(pieces):
        if step is None:
            for src, width, dst, base in jobs:
                for y in range(2):
                    do(
                        pltpu.make_async_copy(
                            piece.at[y, :, pl.ds(src, width)],
                            dst.at[:, pl.ds(base + y * width, width)],
                            sem,
                        )
                    )
            continue
        y, z, c = sp[0], sp[1], sp[2]
        band = parts[1]
        row = pl.multiple_of(
            lax.rem(z + parts[0] - step, parts[0]) * (2 * band) + (c ^ other_c) * band, 16
        )
        for src, width, dst, base in jobs:
            col = pl.multiple_of(base + (y ^ other_y) * width, LANES)
            do(
                pltpu.make_async_copy(
                    piece.at[:, pl.ds(src, width)],
                    dst.at[pl.ds(row, band), pl.ds(col, width)],
                    sem,
                )
            )


def load_pieces(sp, pieces, jobs, sem, parts):
    fetch(sp, pieces, jobs, sem, parts, lambda copy: copy.start())
    fetch(sp, pieces, jobs, sem, parts, lambda copy: copy.wait())


def features_body(layout, sp, x_ref, ln_ref, wf_ref, *rest):
    names, parts = layout
    pieces = list(zip(rest[: len(names)], names))
    a1_ref, qkv_ref, phi_ref, state_ref, full_ref, states, sem = rest[len(names) :]
    step = pl.program_id(0)
    width = a1_ref.shape[1]
    half = width // 2
    pairs = width // LANES

    @pl.when(step == 0)
    def _():
        jobs = [(g * half, half, full_ref, g * width) for g in range(3)]
        load_pieces(sp, pieces, jobs, sem, parts)
        states[...] = jnp.zeros_like(states)

    scaled, _ = normalized(x_ref[0, 0].astype(F32))
    low = (scaled * ln_ref[0:1, :] + ln_ref[1:2, :]).astype(BF)
    a1_ref[...] = low
    qkv_ref[...] = nn(low, full_ref[...]).astype(BF)
    ones = group_ones()
    left = lanes_of((1, LANES)) < HEAD
    for p in range(pairs):
        v = qkv_ref[:, 2 * width + p * LANES : 2 * width + (p + 1) * LANES]
        unit = jnp.ones_like(v)
        values = (jnp.where(left, v, unit), jnp.where(left, unit, v))
        for part in range(2):
            rows = qkv_ref[:, part * width + p * LANES : part * width + (p + 1) * LANES]
            inner = nn(rows, wf_ref[p])
            shifted = []
            for h in range(2):
                own = inner[:, h * FEAT : (h + 1) * FEAT]
                top = jnp.where(
                    left,
                    jnp.max(jnp.where(left, own, -jnp.inf), -1, keepdims=True),
                    jnp.max(jnp.where(left, -jnp.inf, own), -1, keepdims=True),
                )
                shifted.append(own - top)
            grown = jnp.exp(jnp.concatenate(shifted, -1))
            phi = (grown / nn(grown.astype(BF), ones)).astype(BF)
            at = part * 2 * width + p * 2 * FEAT
            phi_ref[:, at : at + 2 * FEAT] = phi
            if part == 1:
                for h in range(2):
                    states[2 * p + h] += tn(phi[:, h * FEAT : (h + 1) * FEAT], values[h])

    @pl.when(step == pl.num_programs(0) - 1)
    def _():
        def put(p, value):
            state_ref[p] = value.astype(BF)

        pack_states(lambda h: states[h], put, pairs, lanes_of((FEAT, LANES)) < HEAD)


def middle_body(layout, sp, x_ref, cot_ref, v_ref, phi_ref, in_ref, ln_ref, *rest):
    names, parts = layout
    pieces = list(zip(rest[: len(names)], names))
    (out_ref, a2_ref, hid_ref, gup_ref, o_ref, gatt_ref, gn_ref, saved_ref, grad_ref, lnsum_ref,
     w_out, w_up, w_down, states, grads, o_wide, inv_den, sums, sem) = rest[len(names) :]
    step = pl.program_id(0)
    width = out_ref.shape[1]
    half = width // 2
    pairs = width // LANES
    hidden = hid_ref.shape[1]
    left = lanes_of((1, LANES)) < HEAD
    square = lanes_of((FEAT, LANES)) < HEAD

    @pl.when(step == 0)
    def _():
        jobs = [
            (0, half, w_out, 0),
            (half, hidden // 2, w_up, 0),
            (half + hidden // 2, hidden // 2, w_down, 0),
        ]
        load_pieces(sp, pieces, jobs, sem, parts)
        grads[...] = jnp.zeros_like(grads)
        sums[...] = jnp.zeros_like(sums)

        def get(p):
            total = in_ref[0, p].astype(F32)
            for k in range(1, in_ref.shape[0]):
                total = total + in_ref[k, p].astype(F32)
            return total

        def put(h, value):
            states[h] = value

        unpack_states(get, put, pairs, square)

    causal = lax.broadcasted_iota(jnp.int32, (TILE, TILE), 0) >= lax.broadcasted_iota(
        jnp.int32, (TILE, TILE), 1
    )
    for p in range(pairs):
        v = v_ref[:, p * LANES : (p + 1) * LANES]
        unit = jnp.ones_like(v)
        both = []
        for h in range(2):
            head = 2 * p + h
            values = jnp.where(left, v, unit) if h == 0 else jnp.where(left, unit, v)
            query = phi_ref[:, head * FEAT : (head + 1) * FEAT]
            key = phi_ref[:, 2 * width + head * FEAT : 2 * width + (head + 1) * FEAT]
            scores = jnp.where(causal, nt(query, key), 0.0).astype(BF)
            state = states[head].astype(BF)
            saved_ref[0, head] = state
            both.append(nn(scores, values) + nn(query, state))
            states[head] += tn(key, values)
        numer = jnp.where(left, both[0], both[1])
        denom = pltpu.roll(jnp.where(left, both[1], both[0]), HEAD, 1)
        inverse = 1.0 / denom
        mixed = numer * inverse
        at = slice(p * LANES, (p + 1) * LANES)
        o_wide[:, at] = mixed
        inv_den[:, at] = inverse
        o_ref[:, at] = mixed.astype(BF)

    middle = x_ref[0, 0].astype(F32) + nt(o_ref[...], w_out[...])
    scaled, inverse = normalized(middle)
    low = (scaled * ln_ref[2:3, :] + ln_ref[3:4, :]).astype(BF)
    a2_ref[...] = low
    cot = cot_ref[0, 0]
    result = middle
    grad_low = jnp.zeros_like(middle)
    chunk = width
    for j in range(hidden // chunk):
        at = slice(j * chunk, (j + 1) * chunk)
        upper = nn(low, w_up[:, at])
        square_up = upper * upper
        bent = jnp.tanh(ROOT * upper * (1.0 + CUBIC * square_up))
        lifted = 0.5 * (1.0 + bent)
        hid = (upper * lifted).astype(BF)
        slope = lifted + 0.5 * ROOT * upper * (1.0 - bent * bent) * (
            1.0 + 3.0 * CUBIC * square_up
        )
        gup = (nn(cot, w_down[:, at]) * slope).astype(BF)
        hid_ref[:, at] = hid
        gup_ref[:, at] = gup
        result = result + nt(hid, w_down[:, at])
        grad_low = grad_low + nt(gup, w_up[:, at])
    out_ref[...] = result.astype(BF)
    grad_mid = cot.astype(F32) + norm_back(grad_low, scaled, inverse, ln_ref[2:3, :])
    sums[0:8] += row_sums(grad_low * scaled)
    sums[8:16] += row_sums(grad_low)
    gatt = grad_mid.astype(BF)
    gatt_ref[...] = gatt
    ones = group_ones()
    go = nn(gatt, w_out[...]).astype(BF).astype(F32)
    for j in range(pairs // 2):
        wide = slice(j * 2 * LANES, (j + 1) * 2 * LANES)
        inv = inv_den[:, wide]
        numer = go[:, wide] * inv
        denom = nn((go[:, wide] * o_wide[:, wide]).astype(BF), ones) * inv * (-1.0 / HEAD)
        for i in range(2):
            p = 2 * j + i
            one = numer[:, i * LANES : (i + 1) * LANES]
            turned = pltpu.roll(denom[:, i * LANES : (i + 1) * LANES], HEAD, 1)
            for h in range(2):
                head = 2 * p + h
                gn = (jnp.where(left, one, turned) if h == 0 else jnp.where(left, turned, one)).astype(BF)
                gn_ref[:, head * LANES : (head + 1) * LANES] = gn
                grads[head] += tn(phi_ref[:, head * FEAT : (head + 1) * FEAT], gn)

    @pl.when(step == pl.num_programs(0) - 1)
    def _():
        def put(p, value):
            grad_ref[p] = value.astype(BF)

        pack_states(lambda h: grads[h], put, pairs, square)
        lnsum_ref[...] = sums[...]


def weight_body(split, lhs_ref, rhs_ref, out_ref, turned):
    @pl.when(pl.program_id(0) == 0)
    def _():
        turned[...] = lhs_ref[...].T

    out_ref[0] = nn(turned[...], rhs_ref[...]).astype(BF)


def back_body(x_ref, gatt_ref, qkv_ref, phi_ref, gn_ref, saved_ref, in_ref, ln_ref, wf_ref, w_ref,
              gin_ref, gqkv_ref, feat_ref, lnsum_ref, grads, feat, sums):
    step = pl.program_id(0)
    width = gin_ref.shape[2]
    pairs = width // LANES
    left = lanes_of((1, LANES)) < HEAD

    @pl.when(step == 0)
    def _():
        feat[...] = jnp.zeros_like(feat)
        sums[...] = jnp.zeros_like(sums)

        def get(p):
            total = in_ref[0, p].astype(F32)
            for k in range(1, in_ref.shape[0]):
                total = total + in_ref[k, p].astype(F32)
            return total

        def put(h, value):
            grads[h] = value

        unpack_states(get, put, pairs, lanes_of((FEAT, LANES)) < HEAD)

    rows = lax.broadcasted_iota(jnp.int32, (TILE, TILE), 0)
    cols = lax.broadcasted_iota(jnp.int32, (TILE, TILE), 1)
    causal = rows >= cols
    turned = rows <= cols
    ones = group_ones()
    for p in range(pairs):
        at = slice(p * LANES, (p + 1) * LANES)
        v = qkv_ref[:, 2 * width + p * LANES : 2 * width + (p + 1) * LANES]
        unit = jnp.ones_like(v)
        grad_values, grad_query, grad_key = [], [], []
        for h in range(2):
            head = 2 * p + h
            span = slice(head * FEAT, (head + 1) * FEAT)
            values = jnp.where(left, v, unit) if h == 0 else jnp.where(left, unit, v)
            query = phi_ref[:, span]
            key = phi_ref[:, 2 * width + head * FEAT : 2 * width + (head + 1) * FEAT]
            gn = gn_ref[:, span]
            ahead = grads[head].astype(BF)
            scores_t = jnp.where(turned, nt(key, query), 0.0).astype(BF)
            grad_scores = jnp.where(causal, nt(gn, values), 0.0).astype(BF)
            grad_scores_t = jnp.where(turned, nt(values, gn), 0.0).astype(BF)
            grad_query.append(nt(gn, saved_ref[0, head]) + nn(grad_scores, key))
            grad_key.append(nn(grad_scores_t, query) + nt(values, ahead))
            grad_values.append(nn(scores_t, gn) + nn(key, ahead))
            grads[head] += tn(query, gn)
        gqkv_ref[:, 2 * width + p * LANES : 2 * width + (p + 1) * LANES] = jnp.where(
            left, grad_values[0], grad_values[1]
        ).astype(BF)
        for part, grad in ((0, grad_query), (1, grad_key)):
            grad = jnp.concatenate(grad, -1)
            phi = phi_ref[:, part * 2 * width + p * 2 * FEAT : part * 2 * width + (p + 1) * 2 * FEAT].astype(F32)
            weighted = phi * grad
            inner = (weighted - phi * nn(weighted.astype(BF), ones)).astype(BF)
            gqkv_ref[:, part * width + p * LANES : part * width + (p + 1) * LANES] = nt(
                inner, wf_ref[p]
            ).astype(BF)
            feat[p] += tn(qkv_ref[:, part * width + p * LANES : part * width + (p + 1) * LANES], inner)

    grad_low = nt(gqkv_ref[...], w_ref[...])
    scaled, inverse = normalized(x_ref[0, 0].astype(F32))
    grad_in = gatt_ref[...].astype(F32) + norm_back(grad_low, scaled, inverse, ln_ref[0:1, :])
    sums[0:8] += row_sums(grad_low * scaled)
    sums[8:16] += row_sums(grad_low)
    gin_ref[0] = grad_in.astype(BF)

    @pl.when(step == pl.num_programs(0) - 1)
    def _():
        feat_ref[...] = feat[...]
        lnsum_ref[...] = sums[...]


def params():
    return pltpu.CompilerParams(
        dimension_semantics=("arbitrary",), vmem_limit_bytes=VMEM_LIMIT
    )


ANY = pl.BlockSpec(memory_space=pl.ANY)


def whole_spec(shape):
    return pl.BlockSpec(shape, lambda i, *_: (0,) * len(shape), pipeline_mode=pl.Buffered(1))


def shaped(shape, kind):
    return jax.ShapeDtypeStruct(shape, kind)


def run_features(sp, x, ln, wf, pieces, names, parts):
    tokens, width = x.shape[2], x.shape[3]
    pairs = width // LANES
    row = lambda n: pl.BlockSpec((TILE, n), lambda i, sp: (i, 0))
    return pl.pallas_call(
        partial(features_body, (names, parts)),
        grid_spec=pltpu.PrefetchScalarGridSpec(
            num_scalar_prefetch=1,
            grid=(tokens // TILE,),
            in_specs=[
                pl.BlockSpec((1, 1, TILE, width), lambda i, sp: (sp[0], 0, i, 0)),
                whole_spec(ln.shape),
                whole_spec(wf.shape),
            ]
            + [ANY] * len(pieces),
            out_specs=[
                row(width),
                row(3 * width),
                row(4 * width),
                whole_spec((pairs + 1, FEAT, LANES)),
                whole_spec((width, 3 * width)),
            ],
            scratch_shapes=[
                pltpu.VMEM((2 * pairs, FEAT, LANES), F32),
                pltpu.SemaphoreType.DMA,
            ],
        ),
        out_shape=[
            shaped((tokens, width), BF),
            shaped((tokens, 3 * width), BF),
            shaped((tokens, 4 * width), BF),
            shaped((pairs + 1, FEAT, LANES), BF),
            shaped((width, 3 * width), BF),
        ],
        compiler_params=params(),
        name="features",
    )(sp, x, ln, wf, *pieces)


def run_middle(sp, x, cot, qkv, phi, incoming, ln, pieces, names, parts, hidden):
    tokens, width = x.shape[2], x.shape[3]
    pairs = width // LANES
    row = lambda n: pl.BlockSpec((TILE, n), lambda i, sp: (i, 0))
    mine = pl.BlockSpec((1, 1, TILE, width), lambda i, sp: (sp[0], 0, i, 0))
    heads = 2 * pairs
    return pl.pallas_call(
        partial(middle_body, (names, parts)),
        grid_spec=pltpu.PrefetchScalarGridSpec(
            num_scalar_prefetch=1,
            grid=(tokens // TILE,),
            in_specs=[
                mine,
                mine,
                pl.BlockSpec((TILE, width), lambda i, sp: (i, 2)),
                row(4 * width),
                whole_spec(incoming.shape),
                whole_spec(ln.shape),
            ]
            + [ANY] * len(pieces),
            out_specs=[
                row(width),
                row(width),
                row(hidden),
                row(hidden),
                row(width),
                row(width),
                row(2 * width),
                pl.BlockSpec((1, heads, FEAT, LANES), lambda i, sp: (i, 0, 0, 0)),
                whole_spec((pairs + 1, FEAT, LANES)),
                whole_spec((16, width)),
            ],
            scratch_shapes=[
                pltpu.VMEM((width, width), BF),
                pltpu.VMEM((width, hidden), BF),
                pltpu.VMEM((width, hidden), BF),
                pltpu.VMEM((heads, FEAT, LANES), F32),
                pltpu.VMEM((heads, FEAT, LANES), F32),
                pltpu.VMEM((TILE, width), F32),
                pltpu.VMEM((TILE, width), F32),
                pltpu.VMEM((16, width), F32),
                pltpu.SemaphoreType.DMA,
            ],
        ),
        out_shape=[
            shaped((tokens, width), BF),
            shaped((tokens, width), BF),
            shaped((tokens, hidden), BF),
            shaped((tokens, hidden), BF),
            shaped((tokens, width), BF),
            shaped((tokens, width), BF),
            shaped((tokens, 2 * width), BF),
            shaped((tokens // TILE, heads, FEAT, LANES), BF),
            shaped((pairs + 1, FEAT, LANES), BF),
            shaped((16, width), F32),
        ],
        compiler_params=params(),
        name="middle",
    )(sp, x, cot, qkv, phi, incoming, ln, *pieces)


def run_weight(lhs, rhs, chunk, groups, name):
    tokens, width = lhs.shape
    total = rhs.shape[1]
    half = total // (2 * groups)
    per = half // chunk

    def place(i):
        group, rest = i // (2 * per), i % (2 * per)
        return (rest // per, 0, group * per + rest % per)

    return pl.pallas_call(
        partial(weight_body, None),
        grid=(total // chunk,),
        in_specs=[
            pl.BlockSpec((tokens, width), lambda i: (0, 0), pipeline_mode=pl.Buffered(1)),
            pl.BlockSpec((tokens, chunk), lambda i: (0, i)),
        ],
        out_specs=pl.BlockSpec((1, width, chunk), place),
        out_shape=shaped((2, width, total // 2), BF),
        scratch_shapes=[pltpu.VMEM((width, tokens), BF)],
        compiler_params=params(),
        name=name,
    )(lhs, rhs)


def run_back(sp, x, gatt, qkv, phi, gn, saved, incoming, ln, wf, w):
    tokens, width = x.shape[2], x.shape[3]
    pairs = width // LANES
    heads = 2 * pairs
    steps = tokens // TILE
    row = lambda n: pl.BlockSpec((TILE, n), lambda i, sp: (steps - 1 - i, 0))

    def body(sp, *refs):
        back_body(*refs)

    return pl.pallas_call(
        body,
        grid_spec=pltpu.PrefetchScalarGridSpec(
            num_scalar_prefetch=1,
            grid=(steps,),
            in_specs=[
                pl.BlockSpec((1, 1, TILE, width), lambda i, sp: (sp[0], 0, steps - 1 - i, 0)),
                row(width),
                row(3 * width),
                row(4 * width),
                row(2 * width),
                pl.BlockSpec((1, heads, FEAT, LANES), lambda i, sp: (steps - 1 - i, 0, 0, 0)),
                whole_spec(incoming.shape),
                whole_spec(ln.shape),
                whole_spec(wf.shape),
                whole_spec(w.shape),
            ],
            out_specs=[
                pl.BlockSpec((1, TILE, width), lambda i, sp: (0, steps - 1 - i, 0)),
                row(3 * width),
                whole_spec((pairs, LANES, 2 * FEAT)),
                whole_spec((16, width)),
            ],
            scratch_shapes=[
                pltpu.VMEM((heads, FEAT, LANES), F32),
                pltpu.VMEM((pairs, LANES, 2 * FEAT), F32),
                pltpu.VMEM((16, width), F32),
            ],
        ),
        out_shape=[
            shaped((1, tokens, width), BF),
            shaped((tokens, 3 * width), BF),
            shaped((pairs, LANES, 2 * FEAT), F32),
            shaped((16, width), F32),
        ],
        compiler_params=params(),
        name="back",
    )(sp, x, gatt, qkv, phi, gn, saved, incoming, ln, wf, w)


def cycle(size, by):
    return [(i, (i + by) % size) for i in range(size)]


def sibling(size):
    return [(i, i ^ 1) for i in range(size)]


def across(size):
    return [(i, i ^ 2) for i in range(size)]


def gather_pieces(own, ring):
    rows, cols = own.shape
    if not ring:
        part = lax.all_gather(own, "fsdp", axis=0, tiled=True)
        return [lax.all_gather(part, "tp", axis=0)], [(None, 0, 0)], None
    size, peers = lax.axis_size("fsdp"), lax.axis_size("ctx")
    band = rows // 2
    c = lax.axis_index("ctx") % 2
    piece = lax.dynamic_slice_in_dim(own, c * band, band, 0)
    pieces, names = [], []
    for k in range(size):
        if k:
            piece = lax.ppermute(piece, "fsdp", cycle(size, 1))
        swapped = lax.ppermute(piece, "tp", sibling(2))
        pieces += [piece, swapped]
        names += [(k, 0, 0), (k, 1, 0)]
    pieces += [lax.ppermute(one, "ctx", sibling(peers)) for one in pieces]
    names += [(k, y, 1) for k, y, _ in names]
    return pieces, names, (size, band)


def reduce_grads(grad):
    _, rows, cols = grad.shape
    size, peers = lax.axis_size("fsdp"), lax.axis_size("ctx")
    ctx, y, z = lax.axis_index("ctx"), lax.axis_index("tp"), lax.axis_index("fsdp")
    c, x = ctx % 2, ctx // 2
    band = rows // (size * 4)
    grad = grad.reshape(2, size, 2, 2, band, cols)
    pick = lambda a, at, axis: lax.dynamic_index_in_dim(a, at, axis, keepdims=False)

    def halve(value, at, axis, name, perm):
        sent = pick(value, 1 - at, axis).astype(BF)
        got = lax.ppermute(sent, name, perm)
        return pick(value, at, axis).astype(F32) + got.astype(F32)

    grad = halve(grad, c, 2, "ctx", sibling(peers)).astype(BF)
    grad = halve(grad, x, 2, "ctx", across(peers)).astype(BF)
    grad = halve(grad, y, 0, "tp", sibling(2)).astype(BF)
    if size == 4:
        total = pick(grad, z, 0).astype(F32)
        for k in range(1, size):
            sent = pick(grad, lax.rem(z + k, size), 0)
            total = total + lax.ppermute(sent, "fsdp", cycle(size, k)).astype(F32)
    else:
        total = lax.psum_scatter(grad, "fsdp", scatter_dimension=0).astype(F32)
    total = total.astype(BF)
    got = lax.ppermute(total, "ctx", across(peers))
    total = jnp.where(x == 0, jnp.stack([total, got]), jnp.stack([got, total]))
    got = lax.ppermute(total, "ctx", sibling(peers))
    total = jnp.where(c == 0, jnp.stack([total, got]), jnp.stack([got, total]))
    return total.reshape(4 * band, cols).astype(F32)


def both_parts(own, y):
    got = lax.ppermute(own, "tp", sibling(2))
    return jnp.where(y == 0, jnp.stack([own, got]), jnp.stack([got, own]))


def on_device(block_input, ln1_gain, ln1_bias, w_qkv, w_feature, w_out, ln2_gain, ln2_bias, w_up,
              w_down, cotangent):
    micro, seqs, tokens, width = block_input.shape
    assert micro == 2 and seqs == 1 and lax.axis_size("tp") == 2 and lax.axis_size("ctx") == 4
    size, peers = lax.axis_size("fsdp"), lax.axis_size("ctx")
    rows = width // size
    hidden = 2 * w_up.shape[1]
    heads = 2 * w_feature.shape[0]
    pairs = heads // 2
    y, z, ctx = lax.axis_index("tp"), lax.axis_index("fsdp"), lax.axis_index("ctx")
    ring = size == 4
    sp = jnp.stack([y, z, ctx % 2]).astype(jnp.int32)

    small = jnp.concatenate(
        [ln1_gain, ln1_bias, ln2_gain, ln2_bias, w_feature.reshape(-1)]
    )
    small = lax.all_gather(small, ("fsdp", "tp")).reshape(size, 2, -1)
    ln = small[:, 0, : 4 * rows].reshape(size, 4, rows).transpose(1, 0, 2).reshape(4, width)
    ln = jnp.concatenate([ln, ln]).astype(F32)
    wf = small[:, :, 4 * rows :].reshape(size, 2, heads // 2, HEAD // size, HEAD)
    wf = wf.transpose(1, 2, 0, 3, 4).reshape(pairs, 2, HEAD, HEAD)
    wf = jnp.concatenate([wf, -wf], -1)
    zero = jnp.zeros_like(wf[:, 0])
    wf = jnp.concatenate(
        [jnp.concatenate([wf[:, 0], zero], -1), jnp.concatenate([zero, wf[:, 1]], -1)], 1
    )

    first, first_names, parts = gather_pieces(w_qkv.reshape(rows, -1), ring)
    rest, rest_names, _ = gather_pieces(jnp.concatenate([w_out.T, w_up, w_down.T], 1), ring)

    a1, qkv, phi, state, w_full = run_features(sp, block_input, ln, wf, first, first_names, parts)

    def shifted(value, sign):
        got = []
        for k in range(1, peers):
            pairs_of = [(i, i + sign * k) for i in range(peers) if 0 <= i + sign * k < peers]
            got.append(lax.ppermute(value, "ctx", pairs_of))
        return jnp.stack(got)

    (out, a2, hid, gup, o, gatt, gn, saved, grad_state, ln2_sums) = run_middle(
        sp, block_input, cotangent, qkv, phi, shifted(state, 1), ln, rest, rest_names, parts, hidden
    )
    block_output = both_parts(out, y).reshape(block_input.shape)
    later = shifted(grad_state, -1)
    cot = lax.dynamic_index_in_dim(cotangent, y, 0, keepdims=False)[0]
    grad_down = run_weight(cot, hid, 512, 1, "grad_down")
    grad_up = run_weight(a2, gup, 512, 1, "grad_up")
    grad_out = run_weight(gatt, o, 384, 1, "grad_out")
    grad_rest = reduce_grads(jnp.concatenate([grad_out, grad_up, grad_down], -1))

    gin, gqkv, feat, ln1_sums = run_back(
        sp, block_input, gatt, qkv, phi, gn, saved, later, ln, wf, w_full
    )
    grad_input = both_parts(gin, y).reshape(block_input.shape)
    grad_qkv = run_weight(a1, gqkv, 384, 3, "grad_qkv")

    feat = feat.reshape(pairs, 2, HEAD, 2, 2, HEAD)
    feat = jnp.stack([feat[:, h, :, h, 0] - feat[:, h, :, h, 1] for h in range(2)], 1)
    feat = feat.reshape(2, heads // 2, size, HEAD // size, HEAD).transpose(0, 2, 1, 3, 4)
    feat = feat.reshape(2, width, -1)
    sums = jnp.concatenate([ln1_sums, ln2_sums]).reshape(4, 8, width).sum(1).T
    sums = jnp.broadcast_to(sums, (2, width, 4))
    extra = jnp.concatenate([feat, sums], -1)
    extra = jnp.pad(extra, ((0, 0), (0, 0), (0, LANES - extra.shape[-1]))).astype(BF)
    last = reduce_grads(jnp.concatenate([grad_qkv, extra], -1))

    half = width // 2
    grad_qkv = last[:, : 3 * half].reshape(w_qkv.shape)
    extra = last[:, 3 * half :]
    count = feat.shape[-1]
    grad_feature = extra[:, :count].reshape(w_feature.shape)
    ln_grads = [extra[:, count + k] for k in range(4)]
    return (
        block_output,
        grad_input,
        ln_grads[0],
        ln_grads[1],
        grad_qkv,
        grad_feature,
        grad_rest[:, :half].T,
        ln_grads[2],
        ln_grads[3],
        grad_rest[:, half : half + hidden // 2],
        grad_rest[:, half + hidden // 2 :].T,
    )


def solution(mesh):
    placed = (
        P(None, "fsdp", "ctx", None),
        P("fsdp"),
        P("fsdp"),
        P("fsdp", None, "tp"),
        P("tp", "fsdp", None),
        P("tp", "fsdp"),
        P("fsdp"),
        P("fsdp"),
        P("fsdp", "tp"),
        P("tp", "fsdp"),
        P(None, "fsdp", "ctx", None),
    )
    return jax.shard_map(
        on_device,
        mesh=mesh,
        in_specs=placed,
        out_specs=(placed[0], placed[0], *placed[1:10]),
        check_vma=False,
    )
```
